32 devices in a mesh: groups: 2 (over y), tile: 4 (over z), chan: 2 (over x), sub: 2 (over core).
Axes of the slice: x: 2, y: 2, z: 4, core: 2. Of those that a mesh axis runs over, the one named last changes fastest.
Arguments:
- canvas: bfloat16 [64, 64, 1280], P(('groups', 'tile'), 'sub'), parts along dimension 0, may hold values from -300 to 300
- thumb: bfloat16 [512, 1280], P(('groups', 'tile')), parts along dimension 0, may hold values from -18 to 18
- ramps: int32 [4, 16], replicated, may hold values from 1 to 8
- t_embed: float32 [5120], P('groups'), parts along dimension 0, may hold values from -3 to 3
- norm_gain: float32 [1280], replicated, may hold values from 0.1 to 1.9
- w_query: bfloat16 [1280, 1280], P(None, 'chan'), may hold values from -0.15625 to 0.15625
- w_key: bfloat16 [1280, 1280], P(None, 'chan'), may hold values from -0.15625 to 0.15625
- w_value: bfloat16 [1280, 1280], P(None, 'chan'), may hold values from -0.15625 to 0.15625
- w_out: bfloat16 [1280, 1280], P('chan'), may hold values from -0.375 to 0.375
Outputs:
- blended: bfloat16 [64, 64, 1280], P(('groups', 'tile'), 'sub', 'chan'), parts along dimension 0
The draws below stay inside these ranges and needn't reach their ends.
There are 2 independent parts, one for each index of `groups`. The reference program is written for one: setup_inputs(seed, part) draws one part's arguments, and reference() takes and returns one part's arrays. A program takes and returns all parts, laid end to end along the dimension named above; an argument that names none is the same for every part. Nothing has to cross between parts.
All inputs are finite; a program needn't handle non-finite values.
Results may differ from the reference program's by a relative error of at most 0.012.
The reference program's roundings to bfloat16 on the way (of `xt`, `normed`, `values`, `weights` and `attended`) count: a program that leaves them out, or rounds other values in their place, can miss the bound.
Values may be sent and summed in bfloat16 or wider, within the bound.
No kernel may reach another device: no remote copies, remote signals or barrier semaphores. Data moves between devices by JAX's collectives and lax.ppermute only.
A program may use at most 128 MiB of HBM per device.

```python
import math
import jax
import jax.numpy as jnp
from jax import lax

C = 1280
HEADS = 20
HD = 64
GROUPS = 32
TH = 8
M = 4
R = 16
H = 32
W = 64
THUMB = 256
N_TILE = 4
N_CHAN = 2


def draw_canvas(key, part):
    key_base = jax.random.fold_in(key, 11)
    key_rows = jax.random.fold_in(key, 12)
    key_cols = jax.random.fold_in(key, 13)
    key_mean = jax.random.fold_in(key, 14)
    key_place = jax.random.fold_in(key, 15)
    key_column = jax.random.fold_in(key, 16)
    key_strength = jax.random.fold_in(key, 17)
    key_magnitude = jax.random.fold_in(key, 18)
    key_signs = jax.random.fold_in(key, 19)
    base = jax.random.normal(key_base, (H, W, C), jnp.float32)
    row_scale = jnp.exp(jax.random.uniform(key_rows, (H, 1, 1), jnp.float32) * math.log(10.0))
    col_pos = lax.iota(jnp.float32, W).reshape(1, W, 1) / W
    col_rough = jnp.exp(jax.random.uniform(key_cols, (1, W, 1), jnp.float32) * math.log(2.0))
    col_scale = (1.0 + 2.0 * col_pos) * col_rough
    values = base * row_scale * col_scale / 4.0
    offset = jax.random.uniform(key_mean, (1, 1, C), jnp.float32, -2.0, 2.0)
    values = values + offset * row_scale * (0.6 + 1.6 * col_pos)
    blocks = H // TH
    spike_row = lax.iota(jnp.int32, blocks) * TH + jax.random.randint(key_place, (blocks,), 0, TH)
    spike_col = jax.random.randint(key_column, (blocks,), 0, W)
    live_block = lax.iota(jnp.int32, blocks) % 4 == 0
    strength = jnp.exp(jax.random.uniform(key_strength, (blocks,), jnp.float32, math.log(40.0), math.log(300.0)))
    magnitude = jax.random.uniform(key_magnitude, (blocks, C), jnp.float32, 0.5, 1.0)
    signs = jnp.where(jax.random.bernoulli(key_signs, 0.5, (blocks, C)), 1.0, -1.0)
    spike_values = strength[:, None] * magnitude * signs
    row_ids = lax.iota(jnp.int32, H)
    col_ids = lax.iota(jnp.int32, W)
    rep_row = jnp.repeat(spike_row, TH)
    rep_col = jnp.repeat(spike_col, TH)
    rep_live = jnp.repeat(live_block, TH)
    rep_values = jnp.repeat(spike_values, TH, axis=0)
    hit = (rep_live & (row_ids == rep_row))[:, None] & (col_ids[None, :] == rep_col[:, None])
    values = jnp.where(hit[:, :, None], rep_values[:, None, :], values)
    values = jnp.clip(values, -300.0, 300.0)
    return values.astype(jnp.bfloat16)


def plant(drawn, rng, low, top_value):
    dims = drawn.shape
    index_at = [jax.random.randint(jax.random.fold_in(rng, axis), (), 0, dims[axis]) for axis in range(len(dims))]
    drawn = drawn.at[tuple(index_at)].set(low)
    longest = dims.index(max(dims))
    index_at[longest] = (index_at[longest] + 1) % dims[longest]
    return drawn.at[tuple(index_at)].set(top_value)


def steps_of(key, dims, split, low, largest):
    factor_of = 1.0
    for dim, shards_of in split:
        draws = jax.random.uniform(jax.random.fold_in(jax.random.fold_in(key, 6), dim), (shards_of,), jnp.float32, low / len(split), largest / len(split))
        factor_of = factor_of * jnp.repeat(jnp.exp(draws), dims[dim] // shards_of).reshape((-1,) + (1,) * (len(dims) - 1 - dim))
    return factor_of


def scatter_about(key, extent, scale, bound, shards=(), held_as=jnp.bfloat16):
    result = jax.random.normal(key, extent, jnp.float32) * scale
    if len(shards) > 0:
        result = steps_of(key, extent, shards, -0.22, 0.18) * result
    return jnp.clip(result, min=-bound, max=bound).astype(held_as)


def setup_inputs(seed: int = 0, part: int = 0) -> dict:
    arg_keys = jax.random.split(jax.random.key(seed), 10)
    part_splits = jax.random.split(jax.random.fold_in(arg_keys[9], part), 10)
    canvas = draw_canvas(jax.random.fold_in(jax.random.fold_in(arg_keys[9], part), 71), part)
    thumb = scatter_about(part_splits[1], (THUMB, C), 3.0, 18.0, ((0, 4),))
    ramps = plant(jax.random.randint(arg_keys[2], (N_TILE, R), 1, 9), jax.random.fold_in(arg_keys[2], 1), 1, 8).astype(jnp.int32)
    t_embed = scatter_about(part_splits[3], (2 * C,), 0.5, 3.0, (), jnp.float32)
    norm_gain = jnp.clip(1.0 + 0.18 * jax.random.normal(arg_keys[4], (C,), jnp.float32), 0.1, 1.9)
    w_query = scatter_about(arg_keys[5], (C, C), C ** -0.5, 0.15625, ((1, 2),))
    w_key = scatter_about(arg_keys[6], (C, C), C ** -0.5, 0.15625, ((1, 2),))
    w_value = scatter_about(arg_keys[7], (C, C), C ** -0.5, 0.15625, ((1, 2),))
    w_out = scatter_about(arg_keys[8], (C, C), (HD * 4) ** -0.5, 0.375, ((0, 2),))
    return {"canvas": canvas, "thumb": thumb, "ramps": ramps, "t_embed": t_embed, "norm_gain": norm_gain, "w_query": w_query, "w_key": w_key, "w_value": w_value, "w_out": w_out}


def reference(canvas, thumb, ramps, t_embed, norm_gain, w_query, w_key, w_value, w_out):
    rows_tile = TH + 2 * M
    padded = jnp.pad(canvas, ((M, M), (0, 0), (0, 0)))
    keys = jnp.dot(thumb, w_key, preferred_element_type=jnp.float32).astype(jnp.bfloat16)
    values = jnp.dot(thumb, w_value, preferred_element_type=jnp.float32).astype(jnp.bfloat16)
    keys3 = keys.astype(jnp.float32).reshape(THUMB, HEADS, HD)
    values3 = values.astype(jnp.float32).reshape(THUMB, HEADS, HD)
    scale = t_embed[:C]
    shift = t_embed[C:]
    width = canvas.shape[1]

    def one_tile(tile_id):
        start = (tile_id * TH).astype(jnp.int32)
        xt = lax.dynamic_slice_in_dim(padded, start, rows_tile, 0).astype(jnp.float32)
        grouped = xt.reshape(rows_tile, width, GROUPS, C // GROUPS)
        mean = lax.optimization_barrier(jnp.mean(grouped, axis=(0, 1, 3)))
        centered = grouped - mean[None, None, :, None]
        var = lax.optimization_barrier(jnp.mean(centered * centered, axis=(0, 1, 3)))
        normed = (centered / jnp.sqrt(var + 1e-05)[None, None, :, None]).reshape(rows_tile, width, C)
        normed = (normed * norm_gain * (1.0 + scale) + shift).astype(jnp.bfloat16)
        query = jnp.dot(normed.reshape(rows_tile * width, C), w_query, preferred_element_type=jnp.float32).astype(jnp.bfloat16)
        query3 = query.astype(jnp.float32).reshape(rows_tile * width, HEADS, HD)
        scores = jnp.einsum('qhd,khd->hqk', query3, keys3) * 0.125
        top = lax.optimization_barrier(jnp.max(scores, axis=-1, keepdims=True))
        expo = jnp.exp(scores - top)
        total = lax.optimization_barrier(jnp.sum(expo, axis=-1))
        weights = expo.astype(jnp.bfloat16).astype(jnp.float32)
        attended = jnp.einsum('hqk,khd->qhd', weights, values3) / jnp.transpose(total)[:, :, None]
        attended = attended.astype(jnp.bfloat16).reshape(rows_tile * width, N_CHAN, C // N_CHAN)
        outw = w_out.astype(jnp.float32).reshape(N_CHAN, C // N_CHAN, C)
        partial_value = jnp.einsum('qcj,cjn->cqn', attended.astype(jnp.float32), outw)
        pred = lax.optimization_barrier(jnp.sum(partial_value.astype(jnp.bfloat16).astype(jnp.float32), axis=0))
        ramp = ramps[tile_id].astype(jnp.float32)
        return pred.reshape(rows_tile, width, C) * ramp[:, None, None]
    weighted = lax.map(one_tile, jnp.arange(N_TILE, dtype=jnp.int32))
    ramp_all = ramps.astype(jnp.float32)
    own = weighted[:, M:M + TH]
    zero_one = jnp.zeros((1, M, width, C), jnp.float32)
    from_above = jnp.concatenate([zero_one, weighted[:-1, M + TH:]], axis=0)
    from_below = jnp.concatenate([weighted[1:, :M], zero_one], axis=0)
    numer = own.at[:, :M].add(from_above).at[:, TH - M:].add(from_below)
    zero_w = jnp.zeros((1, M), jnp.float32)
    w_above = jnp.concatenate([zero_w, ramp_all[:-1, M + TH:]], axis=0)
    w_below = jnp.concatenate([ramp_all[1:, :M], zero_w], axis=0)
    denom = ramp_all[:, M:M + TH].at[:, :M].add(w_above).at[:, TH - M:].add(w_below)
    blended = numer / denom[:, :, None, None]
    return blended.reshape(N_TILE * TH, width, C).astype(jnp.bfloat16)
```

```python
import functools

import jax
import jax.numpy as jnp
from jax import lax
from jax.experimental import pallas as pl
from jax.experimental.pallas import tpu as pltpu
from jax.sharding import PartitionSpec as P

HD = 64
GROUPS = 32
M = 4
LANES = 128
EPS = 1e-05
F32 = jnp.float32
BF16 = jnp.bfloat16
NT = (((1,), (1,)), ((), ()))


def three_parts(v):
    hi = v.astype(BF16).astype(F32)
    rest = v - hi
    mid = rest.astype(BF16).astype(F32)
    return hi, mid, rest - mid


def group_of_channel(channels):
    size = channels // GROUPS
    row = lax.broadcasted_iota(jnp.int32, (LANES, channels), 0)
    col = lax.broadcasted_iota(jnp.int32, (LANES, channels), 1)
    first = row * size
    return jnp.where((col >= first) & (col < first + size), 1.0, 0.0).astype(BF16)


def exact_dot(v, member, dims):
    parts = jnp.concatenate(three_parts(v), axis=0).astype(BF16)
    out = lax.dot_general(parts, member, dims, preferred_element_type=F32)
    return out[0:8] + out[8:16] + out[16:24]


def rows_of(pairs, width):
    row = lax.broadcasted_iota(jnp.int32, (8, width), 0)
    out = jnp.zeros((8, width), F32)
    for i, v in pairs.items():
        out = jnp.where(row == i, jnp.broadcast_to(v, (8, width)), out)
    return out


def local_stats(canvas_ref, thumb_ref, pay_ref, st_ref):
    channels = canvas_ref.shape[1]
    half = pay_ref.shape[0]
    n = canvas_ref.shape[0] // 2
    size = channels // GROUPS
    sub = lax.axis_index("sub")
    start = pl.multiple_of(sub * half, half)
    pay_ref[:, :channels] = thumb_ref[pl.ds(start, half), :]
    means, squares = [], []
    for b in range(2):
        x = canvas_ref[b * n : (b + 1) * n, :].astype(F32)
        mean = jnp.sum(x, axis=0, keepdims=True) * (1.0 / n)
        c = x - mean
        means.append(mean)
        squares.append(jnp.sum(c * c, axis=0, keepdims=True))
    member = group_of_channel(channels)
    mean_g = exact_dot(rows_of({0: means[0], 1: means[1]}, channels), member, NT) * (1.0 / size)
    back = exact_dot(mean_g, member, (((1,), (0,)), ((), ())))
    tot = []
    for b in range(2):
        diff = means[b] - back[b : b + 1]
        tot.append(squares[b] + n * (diff * diff))
    m2_g = exact_dot(rows_of({2: tot[0], 3: tot[1]}, channels), member, NT)
    parts = three_parts(mean_g + m2_g)
    pad = jnp.zeros((half - 24, LANES), F32)
    block = jnp.concatenate(list(parts) + [pad], axis=0).astype(BF16)
    pay_ref[:, channels:] = block
    st_ref[...] = block


def row_weights(ramps_ref, tile, n_tile, columns, upper):
    owned = 2 * M
    shape = (M * columns, 1)
    row = lax.broadcasted_iota(jnp.int32, shape, 0)
    own = jnp.zeros(shape, F32)
    other = jnp.zeros(shape, F32)
    if upper:
        peer, live = jnp.maximum(tile - 1, 0), tile > 0
    else:
        peer, live = jnp.minimum(tile + 1, n_tile - 1), tile < n_tile - 1
    gate = jnp.where(live, 1.0, 0.0).astype(F32)
    for r in range(M):
        here = (row >= r * columns) & (row < (r + 1) * columns)
        own_r = ramps_ref[tile, (M if upper else 2 * M) + r].astype(F32)
        other_r = ramps_ref[peer, (M + owned if upper else 0) + r].astype(F32) * gate
        own = jnp.where(here, own_r, own)
        other = jnp.where(here, other_r, other)
    total = own + other
    return own / total, other / total


def attend(q, k_ref, v_ref, wo_ref, weights, bl_ref, send_ref, own_ref, split):
    n = bl_ref.shape[0]
    w_own, w_other = weights
    width = k_ref.shape[1]
    for j in range(width // LANES):
        cols = slice(j * LANES, (j + 1) * LANES)
        qp = q(cols)
        kp, vp = k_ref[:, cols], v_ref[:, cols]
        low = lax.broadcasted_iota(jnp.int32, kp.shape, 1) < HD
        zero = jnp.zeros_like(kp)
        out = None
        for h in range(2):
            keep = low if h == 0 else jnp.logical_not(low)
            k_h, v_h = jnp.where(keep, kp, zero), jnp.where(keep, vp, zero)
            s = lax.dot_general(qp, k_h, NT, preferred_element_type=F32)
            p = jnp.exp(s - jnp.max(s, axis=1, keepdims=True))
            total = jnp.sum(p, axis=1, keepdims=True)
            o = jnp.dot(p.astype(BF16), v_h, preferred_element_type=F32) * (1.0 / total)
            out = o if out is None else out + o
        att = out.astype(BF16).astype(F32)
        bl_ref[:, cols] = (att[:n] * w_own + att[n:] * w_other).astype(BF16)
    term = jnp.dot(bl_ref[...], wo_ref[...], preferred_element_type=F32)
    if split:
        half = term.shape[1] // 2
        first = lax.axis_index("chan") == 0
        lo, hi = term[:, :half], term[:, half:]
        own_ref[...] = jnp.where(first, lo, hi).astype(BF16)
        send_ref[...] = jnp.where(first, hi, lo).astype(BF16)
    else:
        send_ref[...] = term.astype(BF16)


def merged_stats(stats, tile, n_tile, count, member):
    live = {}
    for o in range(-2, 3):
        ok = (tile + o >= 0) & (tile + o < n_tile)
        gate = jnp.where(ok, 1.0, 0.0).astype(F32)
        live[o] = [v * gate for v in stats[o]]
    rows = {}
    for i, o in enumerate((-1, 0, 1)):
        blocks = []
        for s in range(len(stats[0])):
            blocks += [
                (live[o - 1][s][1:2], live[o - 1][s][3:4]),
                (live[o][s][0:1], live[o][s][2:3]),
                (live[o][s][1:2], live[o][s][3:4]),
                (live[o + 1][s][0:1], live[o + 1][s][2:3]),
            ]
        mean = sum(m for m, _ in blocks) * (1.0 / len(blocks))
        m2 = sum(q for _, q in blocks) + count * sum((m - mean) * (m - mean) for m, _ in blocks)
        rows[i] = mean
        rows[3 + i] = 1.0 / jnp.sqrt(m2 * (1.0 / (count * len(blocks))) + EPS)
    return exact_dot(rows_of(rows, LANES), member, (((1,), (0,)), ((), ())))


def fill_normed(canvas_ref, rows, affine, normed_ref, order):
    chan, gain, shift = affine
    n = normed_ref.shape[0] // 2
    x = canvas_ref[rows, :].astype(F32)
    for i, o in enumerate(order):
        mean, rstd = chan[o + 1 : o + 2], chan[o + 4 : o + 5]
        normed_ref[i * n : (i + 1) * n, :] = ((x - mean) * (rstd * gain) + shift).astype(BF16)


def first_block(n_tile, split, count, columns, *refs):
    (ramps_ref, canvas_ref, thumb_ref, temb_ref, gain_ref, wq_ref, wk_ref, wv_ref, wo_ref, st_ref, st_peer_ref) = refs[:11]
    near = refs[11 : 11 + n_tile - 1]
    far = refs[11 + n_tile - 1 : 11 + 2 * (n_tile - 1)]
    rest = refs[11 + 2 * (n_tile - 1) :]
    if split:
        send_ref, own_ref, k_ref, v_ref, chan_ref, all_ref, normed_ref, q_ref, bl_ref = rest
    else:
        send_ref, k_ref, v_ref, chan_ref, all_ref, normed_ref, q_ref, bl_ref = rest
        own_ref = None
    channels = canvas_ref.shape[1]
    half = near[0].shape[0]
    tile = lax.axis_index("tile")

    def stat(ref, lanes):
        v = ref[:, lanes].astype(F32)
        return v[0:8] + v[8:16] + v[16:24]

    full, tail = slice(0, LANES), slice(channels, channels + LANES)
    stats = {0: [stat(st_ref, full), stat(st_peer_ref, full)]}
    for o in (-2, -1, 1, 2):
        k = (-o) % n_tile
        stats[o] = [stat(near[k - 1], tail), stat(far[k - 1], tail)] if k else stats[0]
    chan = merged_stats(stats, tile, n_tile, float(count), group_of_channel(channels))
    gain = gain_ref[...] * (1.0 + temb_ref[:, :channels])
    shift = temb_ref[:, channels:]
    n = normed_ref.shape[0] // 2
    fill_normed(canvas_ref, slice(0, n), (chan, gain, shift), normed_ref, (0, -1))
    chan_ref[...] = chan
    q_ref[...] = (jnp.dot(normed_ref[...], wq_ref[...], preferred_element_type=F32).astype(BF16)) * 0.125

    own_rows = thumb_ref.shape[0]
    all_ref[:own_rows, :] = thumb_ref[...]
    for i, ref in enumerate(near + far):
        all_ref[own_rows + i * half : own_rows + (i + 1) * half, :] = ref[:, :channels]
    k_ref[...] = jnp.dot(all_ref[...], wk_ref[...], preferred_element_type=F32).astype(BF16)
    v_ref[...] = jnp.dot(all_ref[...], wv_ref[...], preferred_element_type=F32).astype(BF16)
    weights = row_weights(ramps_ref, tile, n_tile, columns, True)
    attend(lambda cols: q_ref[:, cols], k_ref, v_ref, wo_ref, weights, bl_ref, send_ref, own_ref, split)


def second_block(n_tile, split, columns, *refs):
    ramps_ref, canvas_ref, temb_ref, gain_ref, wq_ref, wo_ref, k_ref, v_ref, chan_ref = refs[:9]
    if split:
        send_ref, own_ref, normed_ref, q_ref, bl_ref = refs[9:]
    else:
        send_ref, normed_ref, q_ref, bl_ref = refs[9:]
        own_ref = None
    channels = canvas_ref.shape[1]
    tile = lax.axis_index("tile")
    gain = gain_ref[...] * (1.0 + temb_ref[:, :channels])
    shift = temb_ref[:, channels:]
    n = normed_ref.shape[0] // 2
    fill_normed(canvas_ref, slice(n, 2 * n), (chan_ref[...], gain, shift), normed_ref, (0, 1))
    q_ref[...] = (jnp.dot(normed_ref[...], wq_ref[...], preferred_element_type=F32).astype(BF16)) * 0.125
    weights = row_weights(ramps_ref, tile, n_tile, columns, False)
    attend(lambda cols: q_ref[:, cols], k_ref, v_ref, wo_ref, weights, bl_ref, send_ref, own_ref, split)


def add_up(own_a, got_a, own_b, got_b, out_ref):
    n = own_a.shape[0]
    out_ref[:n, :] = (own_a[...].astype(F32) + got_a[...].astype(F32)).astype(BF16)
    out_ref[n:, :] = (own_b[...].astype(F32) + got_b[...].astype(F32)).astype(BF16)


def shifted(value, axis, step):
    count = lax.axis_size(axis)
    return lax.ppermute(value, axis, [(i, (i + step) % count) for i in range(count)])


def on_device(canvas, thumb, ramps, t_embed, norm_gain, w_query, w_key, w_value, w_out):
    owned, columns, channels = canvas.shape
    n_tile, n_chan, n_sub = (lax.axis_size(a) for a in ("tile", "chan", "sub"))
    assert owned == 2 * M and n_sub == 2
    local_ch = w_query.shape[1]
    width = -(-local_ch // LANES) * LANES
    if width != local_ch:
        grow = width - local_ch
        w_query, w_key, w_value = (jnp.pad(w, ((0, 0), (0, grow))) for w in (w_query, w_key, w_value))
        w_out = jnp.pad(w_out, ((0, grow), (0, 0)))
    rows = owned * columns
    n = rows // 2
    x = canvas.reshape(rows, channels)
    half = thumb.shape[0] // n_sub
    tokens = thumb.shape[0] * n_tile
    count = n * (channels // GROUPS)
    split = n_chan == 2 and (channels // 2) % LANES == 0
    vmem = pl.BlockSpec(memory_space=pltpu.VMEM)
    smem = pl.BlockSpec(memory_space=pltpu.SMEM)

    payload, st = pl.pallas_call(
        local_stats,
        out_shape=(
            jax.ShapeDtypeStruct((half, channels + LANES), BF16),
            jax.ShapeDtypeStruct((half, LANES), BF16),
        ),
        in_specs=[vmem, vmem],
        out_specs=(vmem, vmem),
        name="local_stats",
    )(x, thumb)

    if n_tile <= 4:
        near = [shifted(payload, "tile", k) for k in range(1, n_tile)]
    else:
        every = lax.all_gather(payload, "tile", axis=0)
        me = lax.axis_index("tile")
        near = [lax.dynamic_index_in_dim(every, (me - k) % n_tile, 0, False) for k in range(1, n_tile)]
    st_peer = shifted(st, "sub", 1)
    far = [shifted(v, "sub", 1) for v in near]

    temb = t_embed.reshape(1, -1)
    gain = norm_gain.reshape(1, -1)
    part = jax.ShapeDtypeStruct((n, channels // 2 if split else channels), BF16)
    parts = (part, part) if split else (part,)
    work = [
        pltpu.VMEM((2 * n, channels), BF16),
        pltpu.VMEM((2 * n, width), BF16),
        pltpu.VMEM((n, width), BF16),
    ]
    kv = jax.ShapeDtypeStruct((tokens, width), BF16)
    outs = pl.pallas_call(
        functools.partial(first_block, n_tile, split, count, columns),
        out_shape=parts + (kv, kv, jax.ShapeDtypeStruct((8, channels), F32)),
        in_specs=[smem] + [vmem] * (10 + 2 * (n_tile - 1)),
        out_specs=(vmem,) * (len(parts) + 3),
        scratch_shapes=[pltpu.VMEM((tokens, channels), BF16)] + work,
        name="first_block",
    )(ramps, x, thumb, temb, gain, w_query, w_key, w_value, w_out, st, st_peer, *near, *far)
    first, (keys, values, chan) = outs[: len(parts)], outs[len(parts) :]
    got_a = shifted(first[0], "chan", 1) if split else None
    second = pl.pallas_call(
        functools.partial(second_block, n_tile, split, columns),
        out_shape=parts,
        in_specs=[smem] + [vmem] * 8,
        out_specs=(vmem,) * len(parts),
        scratch_shapes=work,
        name="second_block",
    )(ramps, x, temb, gain, w_query, w_out, keys, values, chan)
    if split:
        got_b = shifted(second[0], "chan", 1)
        out = pl.pallas_call(
            add_up,
            out_shape=jax.ShapeDtypeStruct((rows, channels // 2), BF16),
            in_specs=[vmem] * 4,
            out_specs=vmem,
            name="add_up",
        )(first[1], got_a, second[1], got_b)
    else:
        both = jnp.concatenate([first[0], second[0]], axis=0)
        out = lax.psum_scatter(both, "chan", scatter_dimension=1, tiled=True)
    return out.reshape(owned, columns, out.shape[1])


def solution(mesh):
    placed = (
        P(("groups", "tile"), "sub", None),
        P(("groups", "tile"), None),
        P(),
        P("groups"),
        P(),
        P(None, "chan"),
        P(None, "chan"),
        P(None, "chan"),
        P("chan", None),
    )
    return jax.shard_map(
        on_device,
        mesh=mesh,
        in_specs=placed,
        out_specs=P(("groups", "tile"), "sub", "chan"),
        check_vma=False,
    )
```

```python
import functools

import jax
import jax.numpy as jnp
from jax import lax
from jax.experimental import pallas as pl
from jax.experimental.pallas import tpu as pltpu
from jax.sharding import PartitionSpec as P


HD = 64
GROUPS = 32
M = 4
LANES = 128
EPS = 1e-05
F32 = jnp.float32
BF16 = jnp.bfloat16
NT = (((1,), (1,)), ((), ()))


def three_parts(v):
    hi = v.astype(BF16).astype(F32)
    rest = v - hi
    mid = rest.astype(BF16).astype(F32)
    return hi, mid, rest - mid


def group_of_channel(channels):
    size = channels // GROUPS
    row = lax.broadcasted_iota(jnp.int32, (LANES, channels), 0)
    col = lax.broadcasted_iota(jnp.int32, (LANES, channels), 1)
    first = row * size
    return jnp.where((col >= first) & (col < first + size), 1.0, 0.0).astype(BF16)


def exact_dot(v, member, dims):
    parts = jnp.concatenate(three_parts(v), axis=0).astype(BF16)
    out = lax.dot_general(parts, member, dims, preferred_element_type=F32)
    return out[0:8] + out[8:16] + out[16:24]


def rows_of(pairs, width):
    row = lax.broadcasted_iota(jnp.int32, (8, width), 0)
    out = jnp.zeros((8, width), F32)
    for i, v in pairs.items():
        out = jnp.where(row == i, jnp.broadcast_to(v, (8, width)), out)
    return out


def local_stats(canvas_hbm, thumb_hbm, pay_ref, st_ref, canvas_ref, thumb_ref, sems):
    channels = canvas_ref.shape[1]
    half = pay_ref.shape[0]
    n = canvas_ref.shape[0] // 2
    size = channels // GROUPS
    loads = []
    for b in range(2):
        rows = pl.ds(b * n, n)
        loads.append(pltpu.make_async_copy(canvas_hbm.at[rows], canvas_ref.at[rows], sems.at[b]))
    loads.append(pltpu.make_async_copy(thumb_hbm, thumb_ref, sems.at[2]))
    for load in loads:
        load.start()
    means, squares = [], []
    for b in range(2):
        loads[b].wait()
        x = canvas_ref[b * n : (b + 1) * n, :].astype(F32)
        mean = jnp.sum(x, axis=0, keepdims=True) * (1.0 / n)
        c = x - mean
        means.append(mean)
        squares.append(jnp.sum(c * c, axis=0, keepdims=True))
    member = group_of_channel(channels)
    mean_g = exact_dot(rows_of({0: means[0], 1: means[1]}, channels), member, NT) * (1.0 / size)
    back = exact_dot(mean_g, member, (((1,), (0,)), ((), ())))
    tot = []
    for b in range(2):
        diff = means[b] - back[b : b + 1]
        tot.append(squares[b] + n * (diff * diff))
    m2_g = exact_dot(rows_of({2: tot[0], 3: tot[1]}, channels), member, NT)
    parts = three_parts(mean_g + m2_g)
    pad = jnp.zeros((half - 24, LANES), F32)
    block = jnp.concatenate(list(parts) + [pad], axis=0).astype(BF16)
    pay_ref[:, channels:] = block
    st_ref[...] = block
    loads[2].wait()
    start = pl.multiple_of(lax.axis_index("sub") * half, half)
    pay_ref[:, :channels] = thumb_ref[pl.ds(start, half), :]


def meanwhile(thumb_ref, *refs):
    count = (len(refs) - 3) // 2
    hbm, vmem = refs[:count], refs[count : 2 * count]
    k_ref, v_ref, sems = refs[2 * count :]
    loads = [pltpu.make_async_copy(a, b, sems.at[i]) for i, (a, b) in enumerate(zip(hbm, vmem))]
    for load in loads:
        load.start()
    for i, out in enumerate((k_ref, v_ref)):
        loads[i].wait()
        out[...] = jnp.dot(thumb_ref[...], vmem[i][...], preferred_element_type=F32).astype(BF16)
    for load in loads[2:]:
        load.wait()


def row_weights(ramps_ref, tile, n_tile, columns, upper):
    owned = 2 * M
    shape = (M * columns, 1)
    row = lax.broadcasted_iota(jnp.int32, shape, 0)
    own = jnp.zeros(shape, F32)
    other = jnp.zeros(shape, F32)
    if upper:
        peer, live = jnp.maximum(tile - 1, 0), tile > 0
    else:
        peer, live = jnp.minimum(tile + 1, n_tile - 1), tile < n_tile - 1
    gate = jnp.where(live, 1.0, 0.0).astype(F32)
    for r in range(M):
        here = (row >= r * columns) & (row < (r + 1) * columns)
        own_r = ramps_ref[tile, (M if upper else 2 * M) + r].astype(F32)
        other_r = ramps_ref[peer, (M + owned if upper else 0) + r].astype(F32) * gate
        own = jnp.where(here, own_r, own)
        other = jnp.where(here, other_r, other)
    total = own + other
    return own / total, other / total


def attend(q, k_ref, v_ref, wo_ref, weights, bl_ref, send_ref, own_ref, split):
    n = bl_ref.shape[0]
    w_own, w_other = weights
    width = k_ref.shape[1]
    for j in range(width // LANES):
        cols = slice(j * LANES, (j + 1) * LANES)
        qp = q(cols)
        kp, vp = k_ref[:, cols], v_ref[:, cols]
        low = lax.broadcasted_iota(jnp.int32, kp.shape, 1) < HD
        zero = jnp.zeros_like(kp)
        out = None
        for h in range(2):
            keep = low if h == 0 else jnp.logical_not(low)
            k_h, v_h = jnp.where(keep, kp, zero), jnp.where(keep, vp, zero)
            s = lax.dot_general(qp, k_h, NT, preferred_element_type=F32)
            p = jnp.exp(s - jnp.max(s, axis=1, keepdims=True))
            total = jnp.sum(p, axis=1, keepdims=True)
            o = jnp.dot(p.astype(BF16), v_h, preferred_element_type=F32) * (1.0 / total)
            out = o if out is None else out + o
        att = out.astype(BF16).astype(F32)
        bl_ref[:, cols] = (att[:n] * w_own + att[n:] * w_other).astype(BF16)
    term = jnp.dot(bl_ref[...], wo_ref[...], preferred_element_type=F32)
    if split:
        half = term.shape[1] // 2
        first = lax.axis_index("chan") == 0
        lo, hi = term[:, :half], term[:, half:]
        own_ref[...] = jnp.where(first, lo, hi).astype(BF16)
        send_ref[...] = jnp.where(first, hi, lo).astype(BF16)
    else:
        send_ref[...] = term.astype(BF16)


def merged_stats(stats, tile, n_tile, count, member):
    live = {}
    for o in range(-2, 3):
        ok = (tile + o >= 0) & (tile + o < n_tile)
        gate = jnp.where(ok, 1.0, 0.0).astype(F32)
        live[o] = [v * gate for v in stats[o]]
    rows = {}
    for i, o in enumerate((-1, 0, 1)):
        blocks = []
        for s in range(len(stats[0])):
            blocks += [
                (live[o - 1][s][1:2], live[o - 1][s][3:4]),
                (live[o][s][0:1], live[o][s][2:3]),
                (live[o][s][1:2], live[o][s][3:4]),
                (live[o + 1][s][0:1], live[o + 1][s][2:3]),
            ]
        mean = sum(m for m, _ in blocks) * (1.0 / len(blocks))
        m2 = sum(q for _, q in blocks) + count * sum((m - mean) * (m - mean) for m, _ in blocks)
        rows[i] = mean
        rows[3 + i] = 1.0 / jnp.sqrt(m2 * (1.0 / (count * len(blocks))) + EPS)
    return exact_dot(rows_of(rows, LANES), member, (((1,), (0,)), ((), ())))


def in_one_row(ref, first, last):
    return jnp.concatenate([ref[i : i + 1, :] for i in range(first, last)], axis=1)


def gain_and_shift(temb_ref, gain_ref):
    n = gain_ref.shape[0]
    gain = in_one_row(gain_ref, 0, n) * (1.0 + in_one_row(temb_ref, 0, n))
    return gain, in_one_row(temb_ref, n, 2 * n)


def fill_normed(canvas_ref, rows, affine, normed_ref, order):
    chan, gain, shift = affine
    n = normed_ref.shape[0] // 2
    x = canvas_ref[rows, :].astype(F32)
    for i, o in enumerate(order):
        mean, rstd = chan[o + 1 : o + 2], chan[o + 4 : o + 5]
        normed_ref[i * n : (i + 1) * n, :] = ((x - mean) * (rstd * gain) + shift).astype(BF16)


def first_block(n_tile, split, count, columns, *refs):
    (ramps_ref, canvas_ref, k_own_ref, v_own_ref, temb_ref, gain_ref, wq_ref, wk_ref, wv_ref, wo_ref) = refs[:10]
    st_ref, st_peer_ref = refs[10:12]
    near = refs[12 : 12 + n_tile - 1]
    far = refs[12 + n_tile - 1 : 12 + 2 * (n_tile - 1)]
    rest = refs[12 + 2 * (n_tile - 1) :]
    if split:
        send_ref, own_ref, k_ref, v_ref, chan_ref, all_ref, normed_ref, q_ref, bl_ref = rest
    else:
        send_ref, k_ref, v_ref, chan_ref, all_ref, normed_ref, q_ref, bl_ref = rest
        own_ref = None
    channels = canvas_ref.shape[1]
    half = near[0].shape[0]
    tile = lax.axis_index("tile")

    def stat(ref, lanes):
        v = ref[:, lanes].astype(F32)
        return v[0:8] + v[8:16] + v[16:24]

    full, tail = slice(0, LANES), slice(channels, channels + LANES)
    stats = {0: [stat(st_ref, full), stat(st_peer_ref, full)]}
    for o in (-2, -1, 1, 2):
        k = (-o) % n_tile
        stats[o] = [stat(near[k - 1], tail), stat(far[k - 1], tail)] if k else stats[0]
    chan = merged_stats(stats, tile, n_tile, float(count), group_of_channel(channels))
    gain, shift = gain_and_shift(temb_ref, gain_ref)
    n = normed_ref.shape[0] // 2
    fill_normed(canvas_ref, slice(0, n), (chan, gain, shift), normed_ref, (0, -1))
    chan_ref[...] = chan
    q_ref[...] = (jnp.dot(normed_ref[...], wq_ref[...], preferred_element_type=F32).astype(BF16)) * 0.125

    own_rows = k_own_ref.shape[0]
    for i, ref in enumerate(near + far):
        all_ref[i * half : (i + 1) * half, :] = ref[:, :channels]
    k_ref[:own_rows, :], v_ref[:own_rows, :] = k_own_ref[...], v_own_ref[...]
    k_ref[own_rows:, :] = jnp.dot(all_ref[...], wk_ref[...], preferred_element_type=F32).astype(BF16)
    v_ref[own_rows:, :] = jnp.dot(all_ref[...], wv_ref[...], preferred_element_type=F32).astype(BF16)
    weights = row_weights(ramps_ref, tile, n_tile, columns, True)
    attend(lambda cols: q_ref[:, cols], k_ref, v_ref, wo_ref, weights, bl_ref, send_ref, own_ref, split)


def second_block(n_tile, split, columns, *refs):
    ramps_ref, canvas_ref, temb_ref, gain_ref, wq_ref, wo_ref, k_ref, v_ref, chan_ref = refs[:9]
    if split:
        send_ref, own_ref, normed_ref, q_ref, bl_ref = refs[9:]
    else:
        send_ref, normed_ref, q_ref, bl_ref = refs[9:]
        own_ref = None
    tile = lax.axis_index("tile")
    gain, shift = gain_and_shift(temb_ref, gain_ref)
    n = normed_ref.shape[0] // 2
    fill_normed(canvas_ref, slice(n, 2 * n), (chan_ref[...], gain, shift), normed_ref, (0, 1))
    q_ref[...] = (jnp.dot(normed_ref[...], wq_ref[...], preferred_element_type=F32).astype(BF16)) * 0.125
    weights = row_weights(ramps_ref, tile, n_tile, columns, False)
    attend(lambda cols: q_ref[:, cols], k_ref, v_ref, wo_ref, weights, bl_ref, send_ref, own_ref, split)


def add_up(own_a, got_a, own_b, got_b, out_ref):
    n = own_a.shape[0]
    out_ref[:n, :] = (own_a[...].astype(F32) + got_a[...].astype(F32)).astype(BF16)
    out_ref[n:, :] = (own_b[...].astype(F32) + got_b[...].astype(F32)).astype(BF16)


def resident(*arrays):
    return [pltpu.with_memory_space_constraint(v, pltpu.VMEM) for v in arrays]


def in_hbm(*arrays):
    return [pltpu.with_memory_space_constraint(v, pltpu.HBM) for v in arrays]


def shifted(value, axis, step):
    count = lax.axis_size(axis)
    return lax.ppermute(value, axis, [(i, (i + step) % count) for i in range(count)])


def on_device(canvas, thumb, ramps, t_embed, norm_gain, w_query, w_key, w_value, w_out):
    owned, columns, channels = canvas.shape
    n_tile, n_chan, n_sub = (lax.axis_size(a) for a in ("tile", "chan", "sub"))
    assert owned == 2 * M and n_sub == 2
    local_ch = w_query.shape[1]
    width = -(-local_ch // LANES) * LANES
    if width != local_ch:
        grow = width - local_ch
        w_query, w_key, w_value = (jnp.pad(w, ((0, 0), (0, grow))) for w in (w_query, w_key, w_value))
        w_out = jnp.pad(w_out, ((0, grow), (0, 0)))
    rows = owned * columns
    n = rows // 2
    x = canvas.reshape(rows, channels)
    half = thumb.shape[0] // n_sub
    tokens = thumb.shape[0] * n_tile
    count = n * (channels // GROUPS)
    split = n_chan == 2 and (channels // 2) % LANES == 0
    vmem = pl.BlockSpec(memory_space=pltpu.VMEM)
    smem = pl.BlockSpec(memory_space=pltpu.SMEM)

    hbm = pl.BlockSpec(memory_space=pltpu.HBM)
    payload, st, x, thumb = pl.pallas_call(
        local_stats,
        out_shape=(
            pltpu.VMEM((half, channels + LANES), BF16),
            pltpu.VMEM((half, LANES), BF16),
            pltpu.VMEM(x.shape, BF16),
            pltpu.VMEM(thumb.shape, BF16),
        ),
        in_specs=[hbm, hbm],
        out_specs=(vmem,) * 4,
        scratch_shapes=[pltpu.SemaphoreType.DMA((3,))],
        compiler_params=pltpu.CompilerParams(vmem_limit_bytes=8 << 20),
        name="local_stats",
    )(*in_hbm(x, thumb))
    x, thumb = resident(x, thumb)
    temb = t_embed.reshape(-1, LANES)
    gain = norm_gain.reshape(-1, LANES)
    brought = (w_key, w_value, w_query, w_out, temb, gain)
    own_kv = pltpu.VMEM((thumb.shape[0], width), BF16)
    bring = pl.pallas_call(
        meanwhile,
        out_shape=tuple(pltpu.VMEM(v.shape, v.dtype) for v in brought) + (own_kv, own_kv),
        in_specs=[vmem] + [hbm] * len(brought),
        out_specs=(vmem,) * (len(brought) + 2),
        scratch_shapes=[pltpu.SemaphoreType.DMA((len(brought),))],
        compiler_params=pltpu.CompilerParams(vmem_limit_bytes=8 << 20),
        name="meanwhile",
    )
    *brought, k_own, v_own = bring(thumb, *in_hbm(*brought))
    w_key, w_value, w_query, w_out, temb, gain, k_own, v_own = resident(*brought, k_own, v_own)

    if n_tile <= 4:
        near = [shifted(payload, "tile", k) for k in range(1, n_tile)]
    else:
        every = lax.all_gather(payload, "tile", axis=0)
        me = lax.axis_index("tile")
        near = [lax.dynamic_index_in_dim(every, (me - k) % n_tile, 0, False) for k in range(1, n_tile)]
    st_peer = shifted(st, "sub", 1)
    far = [shifted(v, "sub", 1) for v in near]

    part = pltpu.VMEM((n, channels // 2 if split else channels), BF16)
    parts = (part, part) if split else (part,)
    work = [
        pltpu.VMEM((2 * n, channels), BF16),
        pltpu.VMEM((2 * n, width), BF16),
        pltpu.VMEM((n, width), BF16),
    ]
    kv = pltpu.VMEM((tokens, width), BF16)
    outs = pl.pallas_call(
        functools.partial(first_block, n_tile, split, count, columns),
        out_shape=parts + (kv, kv, pltpu.VMEM((8, channels), F32)),
        in_specs=[smem] + [vmem] * (11 + 2 * (n_tile - 1)),
        out_specs=(vmem,) * (len(parts) + 3),
        scratch_shapes=[pltpu.VMEM((tokens - thumb.shape[0], channels), BF16)] + work,
        compiler_params=pltpu.CompilerParams(vmem_limit_bytes=24 << 20),
        name="first_block",
    )(
        *(ramps, x, k_own, v_own, temb, gain, w_query, w_key, w_value, w_out),
        *resident(st, st_peer, *near, *far),
    )
    first, (keys, values, chan) = outs[: len(parts)], outs[len(parts) :]
    got_a = shifted(first[0], "chan", 1) if split else None
    second = pl.pallas_call(
        functools.partial(second_block, n_tile, split, columns),
        out_shape=parts,
        in_specs=[smem] + [vmem] * 8,
        out_specs=(vmem,) * len(parts),
        scratch_shapes=work,
        compiler_params=pltpu.CompilerParams(vmem_limit_bytes=20 << 20),
        name="second_block",
    )(ramps, x, temb, gain, w_query, w_out, *resident(keys, values, chan))
    if split:
        got_b = shifted(second[0], "chan", 1)
        out = pl.pallas_call(
            add_up,
            out_shape=jax.ShapeDtypeStruct((rows, channels // 2), BF16),
            in_specs=[vmem] * 4,
            out_specs=vmem,
            compiler_params=pltpu.CompilerParams(vmem_limit_bytes=4 << 20),
        name="add_up",
        )(*resident(first[1], got_a, second[1], got_b))
    else:
        both = jnp.concatenate([first[0], second[0]], axis=0)
        out = lax.psum_scatter(both, "chan", scatter_dimension=1, tiled=True)
    return out.reshape(owned, columns, out.shape[1])


def solution(mesh):
    placed = (
        P(("groups", "tile"), "sub", None),
        P(("groups", "tile"), None),
        P(),
        P("groups"),
        P(),
        P(None, "chan"),
        P(None, "chan"),
        P(None, "chan"),
        P("chan", None),
    )
    return jax.shard_map(
        on_device,
        mesh=mesh,
        in_specs=placed,
        out_specs=P(("groups", "tile"), "sub", "chan"),
        check_vma=False,
    )
```

```python
import functools

import jax
import jax.numpy as jnp
from jax import lax
from jax.experimental import pallas as pl
from jax.experimental.pallas import tpu as pltpu
from jax.sharding import PartitionSpec as P


HD = 64
GROUPS = 32
M = 4
LANES = 128
EPS = 1e-05
F32 = jnp.float32
BF16 = jnp.bfloat16
NT = (((1,), (1,)), ((), ()))


def three_parts(v):
    hi = v.astype(BF16).astype(F32)
    rest = v - hi
    mid = rest.astype(BF16).astype(F32)
    return hi, mid, rest - mid


def group_of_channel(channels):
    size = channels // GROUPS
    row = lax.broadcasted_iota(jnp.int32, (GROUPS, channels), 0)
    col = lax.broadcasted_iota(jnp.int32, (GROUPS, channels), 1)
    first = row * size
    some = jnp.where((col >= first) & (col < first + size), 1.0, 0.0).astype(BF16)
    return jnp.concatenate([some, jnp.zeros((LANES - GROUPS, channels), BF16)], axis=0)


def exact_dot(v, member, dims):
    parts = jnp.concatenate(three_parts(v), axis=0).astype(BF16)
    out = lax.dot_general(parts, member, dims, preferred_element_type=F32)
    return out[0:8] + out[8:16] + out[16:24]


def rows_of(pairs, width):
    row = lax.broadcasted_iota(jnp.int32, (8, width), 0)
    out = jnp.zeros((8, width), F32)
    for i, v in pairs.items():
        out = jnp.where(row == i, jnp.broadcast_to(v, (8, width)), out)
    return out


def local_stats(canvas_hbm, thumb_hbm, pay_ref, st_ref, canvas_ref, thumb_ref, sems):
    channels = canvas_ref.shape[1]
    half = pay_ref.shape[0]
    n = canvas_ref.shape[0] // 2
    size = channels // GROUPS
    loads = []
    for b in range(2):
        rows = pl.ds(b * n, n)
        loads.append(pltpu.make_async_copy(canvas_hbm.at[rows], canvas_ref.at[rows], sems.at[b]))
    loads.append(pltpu.make_async_copy(thumb_hbm, thumb_ref, sems.at[2]))
    for load in loads:
        load.start()
    means, squares = [], []
    for b in range(2):
        loads[b].wait()
        mean_parts, square_parts = [], []
        for j in range(channels // LANES):
            x = canvas_ref[b * n : (b + 1) * n, j * LANES : (j + 1) * LANES].astype(F32)
            mean = jnp.sum(x, axis=0, keepdims=True) * (1.0 / n)
            c = x - mean
            mean_parts.append(mean)
            square_parts.append(jnp.sum(c * c, axis=0, keepdims=True))
        means.append(jnp.concatenate(mean_parts, axis=1))
        squares.append(jnp.concatenate(square_parts, axis=1))
    member = group_of_channel(channels)
    mean_g = exact_dot(rows_of({0: means[0], 1: means[1]}, channels), member, NT) * (1.0 / size)
    back = exact_dot(mean_g, member, (((1,), (0,)), ((), ())))
    tot = []
    for b in range(2):
        diff = means[b] - back[b : b + 1]
        tot.append(squares[b] + n * (diff * diff))
    m2_g = exact_dot(rows_of({2: tot[0], 3: tot[1]}, channels), member, NT)
    parts = three_parts(mean_g + m2_g)
    pad = jnp.zeros((half - 24, LANES), F32)
    block = jnp.concatenate(list(parts) + [pad], axis=0).astype(BF16)
    pay_ref[:, channels:] = block
    st_ref[...] = block
    loads[2].wait()
    start = pl.multiple_of(lax.axis_index("sub") * half, half)
    pay_ref[:, :channels] = thumb_ref[pl.ds(start, half), :]


def meanwhile(thumb_ref, *refs):
    count = (len(refs) - 3) // 2
    hbm, vmem = refs[:count], refs[count : 2 * count]
    k_ref, v_ref, sems = refs[2 * count :]
    loads = [pltpu.make_async_copy(a, b, sems.at[i]) for i, (a, b) in enumerate(zip(hbm, vmem))]
    for load in loads:
        load.start()
    for i, out in enumerate((k_ref, v_ref)):
        loads[i].wait()
        out[...] = jnp.dot(thumb_ref[...], vmem[i][...], preferred_element_type=F32).astype(BF16)
    for load in loads[2:]:
        load.wait()


def row_weights(ramps_ref, tile, n_tile, columns, upper):
    owned = 2 * M
    shape = (M * columns, 1)
    row = lax.broadcasted_iota(jnp.int32, shape, 0)
    own = jnp.zeros(shape, F32)
    other = jnp.zeros(shape, F32)
    if upper:
        peer, live = jnp.maximum(tile - 1, 0), tile > 0
    else:
        peer, live = jnp.minimum(tile + 1, n_tile - 1), tile < n_tile - 1
    gate = jnp.where(live, 1.0, 0.0).astype(F32)
    for r in range(M):
        here = (row >= r * columns) & (row < (r + 1) * columns)
        own_r = ramps_ref[tile, (M if upper else 2 * M) + r].astype(F32)
        other_r = ramps_ref[peer, (M + owned if upper else 0) + r].astype(F32) * gate
        own = jnp.where(here, own_r, own)
        other = jnp.where(here, other_r, other)
    total = own + other
    return own / total, other / total


def attend(q, k_ref, v_ref, wo_ref, weights, bl_ref, send_ref, own_ref, split):
    n = bl_ref.shape[0]
    w_own, w_other = weights
    width = k_ref.shape[1]
    for j in range(width // LANES):
        cols = slice(j * LANES, (j + 1) * LANES)
        qp = q(cols)
        kp, vp = k_ref[:, cols], v_ref[:, cols]
        low = lax.broadcasted_iota(jnp.int32, kp.shape, 1) < HD
        zero = jnp.zeros_like(kp)
        out = None
        for h in range(2):
            keep = low if h == 0 else jnp.logical_not(low)
            k_h, v_h = jnp.where(keep, kp, zero), jnp.where(keep, vp, zero)
            s = lax.dot_general(qp, k_h, NT, preferred_element_type=F32)
            p = jnp.exp(s - jnp.max(s, axis=1, keepdims=True))
            total = jnp.sum(p, axis=1, keepdims=True)
            o = jnp.dot(p.astype(BF16), v_h, preferred_element_type=F32) * (1.0 / total)
            out = o if out is None else out + o
        att = out.astype(BF16).astype(F32)
        bl_ref[:, cols] = (att[:n] * w_own + att[n:] * w_other).astype(BF16)
    term = jnp.dot(bl_ref[...], wo_ref[...], preferred_element_type=F32)
    if split:
        half = term.shape[1] // 2
        first = lax.axis_index("chan") == 0
        lo, hi = term[:, :half], term[:, half:]
        own_ref[...] = jnp.where(first, lo, hi).astype(BF16)
        send_ref[...] = jnp.where(first, hi, lo).astype(BF16)
    else:
        send_ref[...] = term.astype(BF16)


def merged_stats(stats, count, member):
    rows = {}
    for i, o in enumerate((-1, 0, 1)):
        blocks = []
        for s in range(len(stats[0])):
            blocks += [
                (stats[o - 1][s][1:2], stats[o - 1][s][3:4]),
                (stats[o][s][0:1], stats[o][s][2:3]),
                (stats[o][s][1:2], stats[o][s][3:4]),
                (stats[o + 1][s][0:1], stats[o + 1][s][2:3]),
            ]
        mean = sum(m for m, _ in blocks) * (1.0 / len(blocks))
        m2 = sum(q for _, q in blocks) + count * sum((m - mean) * (m - mean) for m, _ in blocks)
        rows[i] = mean
        rows[3 + i] = 1.0 / jnp.sqrt(m2 * (1.0 / (count * len(blocks))) + EPS)
    return exact_dot(rows_of(rows, LANES), member, (((1,), (0,)), ((), ())))


def in_one_row(ref, first, last):
    return jnp.concatenate([ref[i : i + 1, :] for i in range(first, last)], axis=1)


def gain_and_shift(temb_ref, gain_ref):
    n = gain_ref.shape[0]
    gain = in_one_row(gain_ref, 0, n) * (1.0 + in_one_row(temb_ref, 0, n))
    return gain, in_one_row(temb_ref, n, 2 * n)


def fill_normed(canvas_ref, rows, affine, normed_ref, order):
    chan, gain, shift = affine
    n = normed_ref.shape[0] // 2
    for j in range(canvas_ref.shape[1] // LANES):
        cols = slice(j * LANES, (j + 1) * LANES)
        x = canvas_ref[rows, cols].astype(F32)
        for i, o in enumerate(order):
            mean, rstd = chan[o + 1 : o + 2, cols], chan[o + 4 : o + 5, cols]
            normed = (x - mean) * (rstd * gain[:, cols]) + shift[:, cols]
            normed_ref[i * n : (i + 1) * n, cols] = normed.astype(BF16)


def first_block(n_tile, split, count, columns, *refs):
    (ramps_ref, canvas_ref, k_own_ref, v_own_ref, temb_ref, gain_ref, wq_ref, wk_ref, wv_ref, wo_ref) = refs[:10]
    st_ref, st_peer_ref = refs[10:12]
    near = refs[12 : 12 + n_tile - 1]
    far = refs[12 + n_tile - 1 : 12 + 2 * (n_tile - 1)]
    rest = refs[12 + 2 * (n_tile - 1) :]
    if split:
        send_ref, own_ref, k_ref, v_ref, chan_ref, all_ref, normed_ref, q_ref, bl_ref = rest
    else:
        send_ref, k_ref, v_ref, chan_ref, all_ref, normed_ref, q_ref, bl_ref = rest
        own_ref = None
    channels = canvas_ref.shape[1]
    half = near[0].shape[0]
    tile = lax.axis_index("tile")

    def stat(ref, lanes):
        v = ref[:, lanes].astype(F32)
        return v[0:8] + v[8:16] + v[16:24]

    full, tail = slice(0, LANES), slice(channels, channels + LANES)
    held = {0: [stat(st_ref, full), stat(st_peer_ref, full)]}
    for k in range(1, n_tile):
        if in_pairs(n_tile) or min(k, n_tile - k) <= 2:
            held[k] = [stat(near[k - 1], tail), stat(far[k - 1], tail)]
    stats = {}
    for o in range(-2, 3):
        stats[o] = [jnp.zeros_like(v) for v in held[0]]
        for k, got in held.items():
            hit = jnp.where(partner(tile, n_tile, k) == tile + o, 1.0, 0.0).astype(F32)
            stats[o] = [a + v * hit for a, v in zip(stats[o], got)]
    chan = merged_stats(stats, float(count), group_of_channel(channels))
    gain, shift = gain_and_shift(temb_ref, gain_ref)
    n = normed_ref.shape[0] // 2
    fill_normed(canvas_ref, slice(0, n), (chan, gain, shift), normed_ref, (0, -1))
    chan_ref[...] = chan
    q_ref[...] = (jnp.dot(normed_ref[...], wq_ref[...], preferred_element_type=F32).astype(BF16)) * 0.125

    own_rows = k_own_ref.shape[0]
    for i, ref in enumerate(near + far):
        all_ref[i * half : (i + 1) * half, :] = ref[:, :channels]
    k_ref[:own_rows, :], v_ref[:own_rows, :] = k_own_ref[...], v_own_ref[...]
    k_ref[own_rows:, :] = jnp.dot(all_ref[...], wk_ref[...], preferred_element_type=F32).astype(BF16)
    v_ref[own_rows:, :] = jnp.dot(all_ref[...], wv_ref[...], preferred_element_type=F32).astype(BF16)
    weights = row_weights(ramps_ref, tile, n_tile, columns, True)
    attend(lambda cols: q_ref[:, cols], k_ref, v_ref, wo_ref, weights, bl_ref, send_ref, own_ref, split)


def second_block(n_tile, split, columns, *refs):
    ramps_ref, canvas_ref, temb_ref, gain_ref, wq_ref, wo_ref, k_ref, v_ref, chan_ref = refs[:9]
    if split:
        send_ref, own_ref, normed_ref, q_ref, bl_ref = refs[9:]
    else:
        send_ref, normed_ref, q_ref, bl_ref = refs[9:]
        own_ref = None
    tile = lax.axis_index("tile")
    gain, shift = gain_and_shift(temb_ref, gain_ref)
    n = normed_ref.shape[0] // 2
    fill_normed(canvas_ref, slice(n, 2 * n), (chan_ref[...], gain, shift), normed_ref, (0, 1))
    q_ref[...] = (jnp.dot(normed_ref[...], wq_ref[...], preferred_element_type=F32).astype(BF16)) * 0.125
    weights = row_weights(ramps_ref, tile, n_tile, columns, False)
    attend(lambda cols: q_ref[:, cols], k_ref, v_ref, wo_ref, weights, bl_ref, send_ref, own_ref, split)


def add_up(own_a, got_a, own_b, got_b, out_ref):
    n = own_a.shape[0]
    out_ref[:n, :] = (own_a[...].astype(F32) + got_a[...].astype(F32)).astype(BF16)
    out_ref[n:, :] = (own_b[...].astype(F32) + got_b[...].astype(F32)).astype(BF16)


def resident(*arrays):
    return [pltpu.with_memory_space_constraint(v, pltpu.VMEM) for v in arrays]


def in_hbm(*arrays):
    return [pltpu.with_memory_space_constraint(v, pltpu.HBM) for v in arrays]


def shifted(value, axis, step):
    count = lax.axis_size(axis)
    return lax.ppermute(value, axis, [(partner(i, count, step), i) for i in range(count)])


def in_pairs(count):
    return count in (1, 2, 4)


def partner(i, count, step):
    return i ^ step if in_pairs(count) else (i - step) % count


def on_device(canvas, thumb, ramps, t_embed, norm_gain, w_query, w_key, w_value, w_out):
    owned, columns, channels = canvas.shape
    n_tile, n_chan, n_sub = (lax.axis_size(a) for a in ("tile", "chan", "sub"))
    assert owned == 2 * M and n_sub == 2
    local_ch = w_query.shape[1]
    width = -(-local_ch // LANES) * LANES
    if width != local_ch:
        grow = width - local_ch
        w_query, w_key, w_value = (jnp.pad(w, ((0, 0), (0, grow))) for w in (w_query, w_key, w_value))
        w_out = jnp.pad(w_out, ((0, grow), (0, 0)))
    rows = owned * columns
    n = rows // 2
    x = canvas.reshape(rows, channels)
    half = thumb.shape[0] // n_sub
    tokens = thumb.shape[0] * n_tile
    count = n * (channels // GROUPS)
    split = n_chan == 2 and (channels // 2) % LANES == 0
    vmem = pl.BlockSpec(memory_space=pltpu.VMEM)
    smem = pl.BlockSpec(memory_space=pltpu.SMEM)

    hbm = pl.BlockSpec(memory_space=pltpu.HBM)
    payload, st, x, thumb = pl.pallas_call(
        local_stats,
        out_shape=(
            pltpu.VMEM((half, channels + LANES), BF16),
            pltpu.VMEM((half, LANES), BF16),
            pltpu.VMEM(x.shape, BF16),
            pltpu.VMEM(thumb.shape, BF16),
        ),
        in_specs=[hbm, hbm],
        out_specs=(vmem,) * 4,
        scratch_shapes=[pltpu.SemaphoreType.DMA((3,))],
        compiler_params=pltpu.CompilerParams(vmem_limit_bytes=8 << 20),
        name="local_stats",
    )(*in_hbm(x, thumb))
    x, thumb = resident(x, thumb)
    temb = t_embed.reshape(-1, LANES)
    gain = norm_gain.reshape(-1, LANES)
    brought = (w_key, w_value, w_query, w_out, temb, gain)
    own_kv = pltpu.VMEM((thumb.shape[0], width), BF16)
    bring = pl.pallas_call(
        meanwhile,
        out_shape=tuple(pltpu.VMEM(v.shape, v.dtype) for v in brought) + (own_kv, own_kv),
        in_specs=[vmem] + [hbm] * len(brought),
        out_specs=(vmem,) * (len(brought) + 2),
        scratch_shapes=[pltpu.SemaphoreType.DMA((len(brought),))],
        compiler_params=pltpu.CompilerParams(vmem_limit_bytes=8 << 20),
        name="meanwhile",
    )
    *brought, k_own, v_own = bring(thumb, *in_hbm(*brought))
    w_key, w_value, w_query, w_out, temb, gain, k_own, v_own = resident(*brought, k_own, v_own)

    if n_tile <= 4:
        near = [shifted(payload, "tile", k) for k in range(1, n_tile)]
    else:
        every = lax.all_gather(payload, "tile", axis=0)
        me = lax.axis_index("tile")
        near = [lax.dynamic_index_in_dim(every, partner(me, n_tile, k), 0, False) for k in range(1, n_tile)]
    st_peer = shifted(st, "sub", 1)
    far = [shifted(v, "sub", 1) for v in near]

    part = pltpu.VMEM((n, channels // 2 if split else channels), BF16)
    parts = (part, part) if split else (part,)
    work = [
        pltpu.VMEM((2 * n, channels), BF16),
        pltpu.VMEM((2 * n, width), BF16),
        pltpu.VMEM((n, width), BF16),
    ]
    kv = pltpu.VMEM((tokens, width), BF16)
    outs = pl.pallas_call(
        functools.partial(first_block, n_tile, split, count, columns),
        out_shape=parts + (kv, kv, pltpu.VMEM((8, channels), F32)),
        in_specs=[smem] + [vmem] * (11 + 2 * (n_tile - 1)),
        out_specs=(vmem,) * (len(parts) + 3),
        scratch_shapes=[pltpu.VMEM((tokens - thumb.shape[0], channels), BF16)] + work,
        compiler_params=pltpu.CompilerParams(vmem_limit_bytes=24 << 20),
        name="first_block",
    )(
        *(ramps, x, k_own, v_own, temb, gain, w_query, w_key, w_value, w_out),
        *resident(st, st_peer, *near, *far),
    )
    first, (keys, values, chan) = outs[: len(parts)], outs[len(parts) :]
    got_a = shifted(first[0], "chan", 1) if split else None
    more = pl.pallas_call(
        functools.partial(second_block, n_tile, split, columns),
        out_shape=parts,
        in_specs=[smem] + [vmem] * 8,
        out_specs=(vmem,) * len(parts),
        scratch_shapes=work,
        compiler_params=pltpu.CompilerParams(vmem_limit_bytes=20 << 20),
        name="second_block",
    )
    second = more(ramps, x, temb, gain, w_query, w_out, *resident(keys, values, chan))
    if split:
        got_b = shifted(second[0], "chan", 1)
        out = pl.pallas_call(
            add_up,
            out_shape=jax.ShapeDtypeStruct((rows, channels // 2), BF16),
            in_specs=[vmem] * 4,
            out_specs=vmem,
            compiler_params=pltpu.CompilerParams(vmem_limit_bytes=4 << 20),
        name="add_up",
        )(*resident(first[1], got_a, second[1], got_b))
    else:
        both = jnp.concatenate([first[0], second[0]], axis=0)
        out = lax.psum_scatter(both, "chan", scatter_dimension=1, tiled=True)
    return out.reshape(owned, columns, out.shape[1])


def solution(mesh):
    placed = (
        P(("groups", "tile"), "sub", None),
        P(("groups", "tile"), None),
        P(),
        P("groups"),
        P(),
        P(None, "chan"),
        P(None, "chan"),
        P(None, "chan"),
        P("chan", None),
    )
    return jax.shard_map(
        on_device,
        mesh=mesh,
        in_specs=placed,
        out_specs=P(("groups", "tile"), "sub", "chan"),
        check_vma=False,
    )
```

```python
import functools

import jax
import jax.numpy as jnp
from jax import lax
from jax.experimental import pallas as pl
from jax.experimental.pallas import tpu as pltpu
from jax.sharding import PartitionSpec as P


HD = 64
GROUPS = 32
M = 4
LANES = 128
EPS = 1e-05
F32 = jnp.float32
BF16 = jnp.bfloat16
CHUNKS = (4, 4)
NT = (((1,), (1,)), ((), ()))


def three_parts(v):
    hi = v.astype(BF16).astype(F32)
    rest = v - hi
    mid = rest.astype(BF16).astype(F32)
    return hi, mid, rest - mid


def group_of_channel(channels):
    size = channels // GROUPS
    row = lax.broadcasted_iota(jnp.int32, (GROUPS, channels), 0)
    col = lax.broadcasted_iota(jnp.int32, (GROUPS, channels), 1)
    first = row * size
    some = jnp.where((col >= first) & (col < first + size), 1.0, 0.0).astype(BF16)
    return jnp.concatenate([some, jnp.zeros((LANES - GROUPS, channels), BF16)], axis=0)


def exact_dot(v, member, dims):
    parts = jnp.concatenate(three_parts(v), axis=0).astype(BF16)
    out = lax.dot_general(parts, member, dims, preferred_element_type=F32)
    return out[0:8] + out[8:16] + out[16:24]


def rows_of(pairs, width):
    row = lax.broadcasted_iota(jnp.int32, (8, width), 0)
    out = jnp.zeros((8, width), F32)
    for i, v in pairs.items():
        out = jnp.where(row == i, jnp.broadcast_to(v, (8, width)), out)
    return out


def local_stats(canvas_hbm, thumb_hbm, pay_ref, st_ref, canvas_ref, thumb_ref, sems):
    channels = canvas_ref.shape[1]
    half = (pay_ref.shape[0] - 16) * LANES // channels
    n = canvas_ref.shape[0] // 2
    size = channels // GROUPS
    loads = []
    for b in range(2):
        rows = pl.ds(b * n, n)
        loads.append(pltpu.make_async_copy(canvas_hbm.at[rows], canvas_ref.at[rows], sems.at[b]))
    loads.append(pltpu.make_async_copy(thumb_hbm, thumb_ref, sems.at[2]))
    for load in loads:
        load.start()
    member = group_of_channel(channels)
    means, squares = [], []
    for b in range(2):
        loads[b].wait()
        mean_parts, square_parts = [], []
        for j in range(channels // LANES):
            x = canvas_ref[b * n : (b + 1) * n, j * LANES : (j + 1) * LANES].astype(F32)
            mean = jnp.sum(x, axis=0, keepdims=True) * (1.0 / n)
            c = x - mean
            mean_parts.append(mean)
            square_parts.append(jnp.sum(c * c, axis=0, keepdims=True))
        means.append(jnp.concatenate(mean_parts, axis=1))
        squares.append(jnp.concatenate(square_parts, axis=1))
    mean_g = exact_dot(rows_of({0: means[0], 1: means[1]}, channels), member, NT) * (1.0 / size)
    back = exact_dot(mean_g, member, (((1,), (0,)), ((), ())))
    tot = []
    for b in range(2):
        diff = means[b] - back[b : b + 1]
        tot.append(squares[b] + n * (diff * diff))
    m2_g = exact_dot(rows_of({2: tot[0], 3: tot[1]}, channels), member, NT)
    hi, mid, lo = three_parts(mean_g + m2_g)
    block = jnp.concatenate([hi + pltpu.roll(mid, 4, axis=0), lo], axis=0).astype(BF16)
    top = pay_ref.shape[0] - 16
    pay_ref[top:, :] = block
    st_ref[...] = block
    loads[2].wait()
    start = pl.multiple_of(lax.axis_index("sub") * half, half)
    for j in range(channels // LANES):
        pay_ref[j * half : (j + 1) * half, :] = thumb_ref[pl.ds(start, half), j * LANES : (j + 1) * LANES]


def meanwhile(thumb_ref, *refs):
    count = (len(refs) - 3) // 2
    hbm, vmem = refs[:count], refs[count : 2 * count]
    k_ref, v_ref, sems = refs[2 * count :]
    loads = [pltpu.make_async_copy(a, b, sems.at[i]) for i, (a, b) in enumerate(zip(hbm, vmem))]
    for load in loads:
        load.start()
    for i, out in enumerate((k_ref, v_ref)):
        loads[i].wait()
        out[...] = jnp.dot(thumb_ref[...], vmem[i][...], preferred_element_type=F32).astype(BF16)
    for load in loads[2:]:
        load.wait()


def row_weights(ramps_ref, tile, n_tile, columns, rows):
    shape = (len(rows) * columns, 1)
    place = lax.broadcasted_iota(jnp.int32, shape, 0)
    own = jnp.zeros(shape, F32)
    other = jnp.zeros(shape, F32)
    for i, r in enumerate(rows):
        here = (place >= i * columns) & (place < (i + 1) * columns)
        if r < M:
            peer, live, at = jnp.maximum(tile - 1, 0), tile > 0, 3 * M + r
        else:
            peer, live, at = jnp.minimum(tile + 1, n_tile - 1), tile < n_tile - 1, r - M
        other_r = ramps_ref[peer, at].astype(F32) * jnp.where(live, 1.0, 0.0).astype(F32)
        own = jnp.where(here, ramps_ref[tile, M + r].astype(F32), own)
        other = jnp.where(here, other_r, other)
    total = own + other
    return own / total, other / total


def masked_keys(k, out_ref):
    zero = jnp.zeros((k.shape[0], LANES), BF16)
    low = lax.broadcasted_iota(jnp.int32, zero.shape, 1) < HD
    for j in range(k.shape[1] // LANES):
        pair = k[:, j * LANES : (j + 1) * LANES]
        out_ref[:, 2 * j * LANES : (2 * j + 1) * LANES] = jnp.where(low, pair, zero)
        out_ref[:, (2 * j + 1) * LANES : (2 * j + 2) * LANES] = jnp.where(low, zero, pair)


def attend(q, k_ref, v_ref, wo_ref, weights, bl_ref, send_ref, own_ref, split):
    n = bl_ref.shape[0]
    w_own, w_other = weights
    width = v_ref.shape[1]
    left = lax.broadcasted_iota(jnp.int32, (2 * n, LANES), 1) < HD
    for j in range(width // LANES):
        cols = slice(j * LANES, (j + 1) * LANES)
        qp, vp = q(cols), v_ref[:, cols]
        outs = []
        for h in range(2):
            k_h = k_ref[:, (2 * j + h) * LANES : (2 * j + h + 1) * LANES]
            s = lax.dot_general(qp, k_h, NT, preferred_element_type=F32)
            p = jnp.exp(s - jnp.max(s, axis=1, keepdims=True))
            total = jnp.sum(p, axis=1, keepdims=True)
            outs.append(jnp.dot(p.astype(BF16), vp, preferred_element_type=F32) * (1.0 / total))
        out = jnp.where(left, outs[0], outs[1])
        att = out.astype(BF16).astype(F32)
        bl_ref[:, cols] = (att[:n] * w_own + att[n:] * w_other).astype(BF16)
    term = jnp.dot(bl_ref[...], wo_ref[...], preferred_element_type=F32)
    if split:
        half = term.shape[1] // 2
        first = lax.axis_index("chan") == 0
        lo, hi = term[:, :half], term[:, half:]
        own_ref[...] = jnp.where(first, lo, hi).astype(BF16)
        send_ref[...] = jnp.where(first, hi, lo).astype(BF16)
    else:
        send_ref[...] = term.astype(BF16)


def merged_stats(stats, count, member):
    rows = {}
    for i, o in enumerate((-1, 0, 1)):
        blocks = []
        for s in range(len(stats[0])):
            blocks += [
                (stats[o - 1][s][1:2], stats[o - 1][s][3:4]),
                (stats[o][s][0:1], stats[o][s][2:3]),
                (stats[o][s][1:2], stats[o][s][3:4]),
                (stats[o + 1][s][0:1], stats[o + 1][s][2:3]),
            ]
        mean = sum(m for m, _ in blocks) * (1.0 / len(blocks))
        m2 = sum(q for _, q in blocks) + count * sum((m - mean) * (m - mean) for m, _ in blocks)
        rows[i] = mean
        rows[3 + i] = 1.0 / jnp.sqrt(m2 * (1.0 / (count * len(blocks))) + EPS)
    return exact_dot(rows_of(rows, LANES), member, (((1,), (0,)), ((), ())))


def in_one_row(ref, first, last):
    return jnp.concatenate([ref[i : i + 1, :] for i in range(first, last)], axis=1)


def gain_and_shift(temb_ref, gain_ref):
    n = gain_ref.shape[0]
    gain = in_one_row(gain_ref, 0, n) * (1.0 + in_one_row(temb_ref, 0, n))
    return gain, in_one_row(temb_ref, n, 2 * n)


def fill_normed(canvas_ref, rows, columns, affine, normed_ref):
    chan, gain, shift = affine
    n = len(rows) * columns
    upper = sum(r < M for r in rows) * columns
    base = rows[0] * columns
    runs = [(0, n, 0, 0), (0, upper, n, -1), (upper, n, n, 1)]
    for j in range(canvas_ref.shape[1] // LANES):
        cols = slice(j * LANES, (j + 1) * LANES)
        for first, last, to, o in runs:
            if last > first:
                x = canvas_ref[base + first : base + last, cols].astype(F32)
                mean, rstd = chan[o + 1 : o + 2, cols], chan[o + 4 : o + 5, cols]
                normed = (x - mean) * (rstd * gain[:, cols]) + shift[:, cols]
                normed_ref[to + first : to + last, cols] = normed.astype(BF16)


def first_block(n_tile, split, count, columns, rows, *refs):
    (ramps_ref, canvas_ref, k_own_ref, v_own_ref, temb_ref, gain_ref, wq_ref, wk_ref, wv_ref, wo_ref) = refs[:10]
    st_ref, st_peer_ref = refs[10:12]
    near = refs[12 : 12 + n_tile - 1]
    far = refs[12 + n_tile - 1 : 12 + 2 * (n_tile - 1)]
    rest = refs[12 + 2 * (n_tile - 1) :]
    if split:
        send_ref, own_ref, k_ref, v_ref, chan_ref, all_ref, normed_ref, q_ref, bl_ref = rest
    else:
        send_ref, k_ref, v_ref, chan_ref, all_ref, normed_ref, q_ref, bl_ref = rest
        own_ref = None
    channels = canvas_ref.shape[1]
    half = (near[0].shape[0] - 16) * LANES // channels
    tile = lax.axis_index("tile")

    def stat(ref):
        v = ref[ref.shape[0] - 16 :, :].astype(F32)
        return v[0:8] + pltpu.roll(v[0:8], 4, axis=0) + v[8:16]

    held = {0: [stat(st_ref), stat(st_peer_ref)]}
    for k in range(1, n_tile):
        if in_pairs(n_tile) or min(k, n_tile - k) <= 2:
            held[k] = [stat(near[k - 1]), stat(far[k - 1])]
    stats = {}
    for o in range(-2, 3):
        stats[o] = [jnp.zeros_like(v) for v in held[0]]
        for k, got in held.items():
            hit = jnp.where(partner(tile, n_tile, k) == tile + o, 1.0, 0.0).astype(F32)
            stats[o] = [a + v * hit for a, v in zip(stats[o], got)]
    chan = merged_stats(stats, float(count), group_of_channel(channels))
    gain, shift = gain_and_shift(temb_ref, gain_ref)
    fill_normed(canvas_ref, rows, columns, (chan, gain, shift), normed_ref)
    chan_ref[...] = chan
    q_ref[...] = (jnp.dot(normed_ref[...], wq_ref[...], preferred_element_type=F32).astype(BF16)) * 0.125

    own_rows = k_own_ref.shape[0]
    for i, ref in enumerate(near + far):
        for j in range(channels // LANES):
            all_ref[i * half : (i + 1) * half, j * LANES : (j + 1) * LANES] = ref[j * half : (j + 1) * half, :]
    v_ref[:own_rows, :] = v_own_ref[...]
    masked_keys(k_own_ref[...], k_ref.at[:own_rows, :])
    masked_keys(jnp.dot(all_ref[...], wk_ref[...], preferred_element_type=F32).astype(BF16), k_ref.at[own_rows:, :])
    v_ref[own_rows:, :] = jnp.dot(all_ref[...], wv_ref[...], preferred_element_type=F32).astype(BF16)
    weights = row_weights(ramps_ref, tile, n_tile, columns, rows)
    attend(lambda cols: q_ref[:, cols], k_ref, v_ref, wo_ref, weights, bl_ref, send_ref, own_ref, split)


def next_block(n_tile, split, columns, rows, *refs):
    ramps_ref, canvas_ref, temb_ref, gain_ref, wq_ref, wo_ref, k_ref, v_ref, chan_ref = refs[:9]
    if split:
        send_ref, own_ref, normed_ref, q_ref, bl_ref = refs[9:]
    else:
        send_ref, normed_ref, q_ref, bl_ref = refs[9:]
        own_ref = None
    tile = lax.axis_index("tile")
    gain, shift = gain_and_shift(temb_ref, gain_ref)
    fill_normed(canvas_ref, rows, columns, (chan_ref[...], gain, shift), normed_ref)
    q_ref[...] = (jnp.dot(normed_ref[...], wq_ref[...], preferred_element_type=F32).astype(BF16)) * 0.125
    weights = row_weights(ramps_ref, tile, n_tile, columns, rows)
    attend(lambda cols: q_ref[:, cols], k_ref, v_ref, wo_ref, weights, bl_ref, send_ref, own_ref, split)


def add_up(places, *refs):
    out_ref, sum_ref, sem = refs[-3:]
    base, length = places[0][0], sum(n for _, n in places)
    for i, (first, n) in enumerate(places):
        total = refs[2 * i][...].astype(F32) + refs[2 * i + 1][...].astype(F32)
        sum_ref[first - base : first - base + n, :] = total.astype(BF16)
    write = pltpu.make_async_copy(sum_ref, out_ref.at[pl.ds(base, length)], sem)
    write.start()
    write.wait()


def resident(*arrays):
    return [pltpu.with_memory_space_constraint(v, pltpu.VMEM) for v in arrays]


def in_hbm(*arrays):
    return [pltpu.with_memory_space_constraint(v, pltpu.HBM) for v in arrays]


def shifted(value, axis, step):
    count = lax.axis_size(axis)
    return lax.ppermute(value, axis, [(partner(i, count, step), i) for i in range(count)])


def in_pairs(count):
    return count in (1, 2, 4)


def partner(i, count, step):
    return i ^ step if in_pairs(count) else (i - step) % count


def on_device(canvas, thumb, ramps, t_embed, norm_gain, w_query, w_key, w_value, w_out):
    owned, columns, channels = canvas.shape
    n_tile, n_chan, n_sub = (lax.axis_size(a) for a in ("tile", "chan", "sub"))
    assert owned == 2 * M and n_sub == 2
    local_ch = w_query.shape[1]
    width = -(-local_ch // LANES) * LANES
    if width != local_ch:
        grow = width - local_ch
        w_query, w_key, w_value = (jnp.pad(w, ((0, 0), (0, grow))) for w in (w_query, w_key, w_value))
        w_out = jnp.pad(w_out, ((0, grow), (0, 0)))
    rows_all = owned * columns
    n = rows_all // 2
    x = canvas.reshape(rows_all, channels)
    half = thumb.shape[0] // n_sub
    tokens = thumb.shape[0] * n_tile
    count = n * (channels // GROUPS)
    split = n_chan == 2 and (channels // 2) % LANES == 0
    vmem = pl.BlockSpec(memory_space=pltpu.VMEM)
    smem = pl.BlockSpec(memory_space=pltpu.SMEM)

    hbm = pl.BlockSpec(memory_space=pltpu.HBM)
    payload, st, x, thumb = pl.pallas_call(
        local_stats,
        out_shape=(
            pltpu.VMEM((half * channels // LANES + 16, LANES), BF16),
            pltpu.VMEM((16, LANES), BF16),
            pltpu.VMEM(x.shape, BF16),
            pltpu.VMEM(thumb.shape, BF16),
        ),
        in_specs=[hbm, hbm],
        out_specs=(vmem,) * 4,
        scratch_shapes=[pltpu.SemaphoreType.DMA((3,))],
        compiler_params=pltpu.CompilerParams(vmem_limit_bytes=8 << 20),
        name="local_stats",
    )(*in_hbm(x, thumb))
    x, thumb = resident(x, thumb)
    temb = t_embed.reshape(-1, LANES)
    gain = norm_gain.reshape(-1, LANES)
    brought = (w_key, w_value, w_query, w_out, temb, gain)
    own_kv = pltpu.VMEM((thumb.shape[0], width), BF16)
    bring = pl.pallas_call(
        meanwhile,
        out_shape=tuple(pltpu.VMEM(v.shape, v.dtype) for v in brought) + (own_kv, own_kv),
        in_specs=[vmem] + [hbm] * len(brought),
        out_specs=(vmem,) * (len(brought) + 2),
        scratch_shapes=[pltpu.SemaphoreType.DMA((len(brought),))],
        compiler_params=pltpu.CompilerParams(vmem_limit_bytes=8 << 20),
        name="meanwhile",
    )
    *brought, k_own, v_own = bring(thumb, *in_hbm(*brought))
    w_key, w_value, w_query, w_out, temb, gain, k_own, v_own = resident(*brought, k_own, v_own)

    if n_tile <= 4:
        near = [shifted(payload, "tile", k) for k in range(1, n_tile)]
    else:
        every = lax.all_gather(payload, "tile", axis=0)
        me = lax.axis_index("tile")
        near = [lax.dynamic_index_in_dim(every, partner(me, n_tile, k), 0, False) for k in range(1, n_tile)]
    st_peer = shifted(st, "sub", 1)
    far = [shifted(v, "sub", 1) for v in near]

    blocks, places, first_row = [], [], 0
    for size in CHUNKS:
        blocks.append(tuple(range(first_row, first_row + size)))
        places.append((first_row * columns, size * columns))
        first_row += size

    def results(rows):
        part = pltpu.VMEM((len(rows) * columns, channels // 2 if split else channels), BF16)
        return (part, part) if split else (part,)

    def work(rows):
        size = len(rows) * columns
        return [pltpu.VMEM((2 * size, channels), BF16), pltpu.VMEM((2 * size, width), BF16), pltpu.VMEM((size, width), BF16)]

    kv = pltpu.VMEM((tokens, width), BF16)
    parts = results(blocks[0])
    outs = pl.pallas_call(
        functools.partial(first_block, n_tile, split, count, columns, blocks[0]),
        out_shape=parts + (pltpu.VMEM((tokens, 2 * width), BF16), kv, pltpu.VMEM((8, channels), F32)),
        in_specs=[smem] + [vmem] * (11 + 2 * (n_tile - 1)),
        out_specs=(vmem,) * (len(parts) + 3),
        scratch_shapes=[pltpu.VMEM((tokens - thumb.shape[0], channels), BF16)] + work(blocks[0]),
        compiler_params=pltpu.CompilerParams(vmem_limit_bytes=24 << 20),
        name="first_block",
    )(
        *(ramps, x, k_own, v_own, temb, gain, w_query, w_key, w_value, w_out),
        *resident(st, st_peer, *near, *far),
    )
    kept = resident(*outs[len(parts) :])
    done = [outs[: len(parts)]]
    got = [shifted(done[0][0], "chan", 1)] if split else []
    for i, rows in enumerate(blocks[1:], 1):
        block = pl.pallas_call(
            functools.partial(next_block, n_tile, split, columns, rows),
            out_shape=results(rows),
            in_specs=[smem] + [vmem] * 8,
            out_specs=(vmem,) * len(parts),
            scratch_shapes=work(rows),
            compiler_params=pltpu.CompilerParams(vmem_limit_bytes=20 << 20),
        )
        done.append(block(ramps, x, temb, gain, w_query, w_out, *kept))
        if split:
            got.append(shifted(done[i][0], "chan", 1))
    if not split:
        both = jnp.concatenate([d[0] for d in done], axis=0)
        out = lax.psum_scatter(both, "chan", scatter_dimension=1, tiled=True)
        return out.reshape(owned, columns, out.shape[1])

    def added(span, into):
        pairs = [v for i in span for v in (done[i][1], got[i])]
        length = sum(places[i][1] for i in span)
        earlier = [] if into is None else in_hbm(into)
        return pl.pallas_call(
            functools.partial(add_up, tuple(places[i] for i in span)),
            out_shape=jax.ShapeDtypeStruct((rows_all, channels // 2), BF16),
            in_specs=[vmem] * len(pairs) + [hbm] * len(earlier),
            out_specs=hbm,
            scratch_shapes=[pltpu.VMEM((length, channels // 2), BF16), pltpu.SemaphoreType.DMA],
            input_output_aliases={len(pairs): 0} if earlier else {},
            compiler_params=pltpu.CompilerParams(vmem_limit_bytes=4 << 20),
        )(*resident(*pairs), *earlier)

    last = len(blocks) - 1
    out = added(range(last), None)
    out = added(range(last, last + 1), out)
    return out.reshape(owned, columns, out.shape[1])


def solution(mesh):
    placed = (
        P(("groups", "tile"), "sub", None),
        P(("groups", "tile"), None),
        P(),
        P("groups"),
        P(),
        P(None, "chan"),
        P(None, "chan"),
        P(None, "chan"),
        P("chan", None),
    )
    return jax.shard_map(
        on_device,
        mesh=mesh,
        in_specs=placed,
        out_specs=P(("groups", "tile"), "sub", "chan"),
        check_vma=False,
    )
```
